256 devices in a mesh: gx: 16 (over x_lo, z), ma: 16 (over y, x_hi, core).
Axes of the slice: x: 4 (x_hi: 2, x_lo: 2; x = x_hi * 2 + x_lo), y: 4, z: 8, core: 2. Of those that a mesh axis runs over, the one named last changes fastest.
Arguments:
- solution: float32 [256, 16, 8, 256], P('ma', 'gx'), may hold values from -1.2 to 1.2
- source: float32 [256, 16, 8, 256], P('ma', 'gx'), may hold values from -6 to 6
- mean_conductivity: float32 [16, 8, 256], P('gx'), may hold values from 0.5 to 2
- kl_fields: float32 [10, 16, 8, 256], P(None, 'gx'), may hold values from -0.9 to 0.9
- couplings: int32 [10, 256, 2], replicated, may hold values from 0 to 255, as said below
- mode_index: int32 [256, 10], replicated, may hold values from 0 to 3, as said below
Outputs:
- residual: float32 [256, 16, 8, 256], P('ma', 'gx')
- correction: float32 [256, 16, 8, 256], P('ma', 'gx')
The draws below stay inside these ranges and needn't reach their ends.
Inputs may be any that keep to these rules, and one draw needn't show every extreme that they name: couplings[k, i, 0] is the mode whose multi-index is mode_index[i] plus one in variable k, couplings[k, i, 1] the mode whose multi-index is mode_index[i] minus one in variable k; where no mode has that multi-index the entry is i itself. `mode_index`: the rows are 256 distinct multi-indices of total degree at most 3 in graded order: the total degree never falls with the mode number, all multi-indices of each total degree below 3 are present, and some mode has degree 3 in one variable; the order of the variables is drawn from the seed.
All inputs are finite; a program needn't handle non-finite values.
Results may differ from the reference program's by a relative error of at most 0.000071.
Values sent between devices are 32-bit elements; how exact they have to be, the bound alone decides.
No kernel may reach another device: no remote copies, remote signals or barrier semaphores. Data moves between devices by JAX's collectives and lax.ppermute only.
A program may use at most 128 MiB of HBM per device.

```python
import jax
import jax.numpy as jnp
import numpy as np
from jax import lax

NY = 8
NZ = 256
P_SIZE = 256
KL = 10
DEG = 3
S = 2
STEPS = 3
NX = 16


def basis_table():
    entries = [[]]
    for variable in range(KL):
        extended = []
        for entry in entries:
            for levels in range(DEG - sum(entry) + 1):
                extended.append(entry + [levels])
        entries = extended
    entries.sort(key=lambda entry: (sum(entry), [-level_value for level_value in entry]))
    return np.array(entries[:P_SIZE], dtype=np.int32)


def chaos_tables(key):
    basis = jnp.asarray(basis_table())
    variable_order = jax.random.permutation(jax.random.fold_in(key, 7), KL)
    indices = jnp.take(basis, variable_order, axis=1).astype(jnp.int32)
    unit_steps = jnp.eye(KL, dtype=jnp.int32)
    mode_ids = jnp.arange(P_SIZE, dtype=jnp.int32)
    partners = []
    for shifted in (1, -1):
        target = indices[None, :, :] + shifted * unit_steps[:, None, :]
        matches = jnp.all(target[:, :, None, :] == indices[None, None, :, :], axis=-1)
        present = jnp.any(matches, axis=-1)
        located = jnp.sum(matches.astype(jnp.int32) * mode_ids[None, None, :], axis=-1)
        partners.append(jnp.where(present, located, jnp.broadcast_to(mode_ids[None, :], located.shape)))
    return (indices, jnp.stack(partners, -1).astype(jnp.int32))


def draw_couplings(key, part):
    return chaos_tables(key)[1]


def draw_mode_index(key, part):
    return chaos_tables(key)[0]


def steps_of(rng, shape, cuts, least, high):
    def one(dim, parts):
        steps = jax.random.uniform(jax.random.fold_in(jax.random.fold_in(rng, 6), dim), (parts,), jnp.float32, least / len(cuts), high / len(cuts))
        return jnp.repeat(jnp.exp(steps), shape[dim] // parts).reshape((-1,) + (1,) * (len(shape) - dim - 1))

    loudness = one(*cuts[0])
    for cut in cuts[1:]:
        loudness = loudness * one(*cut)
    return loudness


def bell_draw(key, shape, spread, bound, shards=(), kind=jnp.bfloat16):
    drawn = jax.random.normal(key, shape, jnp.float32) * spread
    if len(shards) > 0:
        drawn = steps_of(key, shape, shards, -0.22, 0.18) * drawn
    return jnp.clip(drawn, min=-bound, max=bound).astype(kind)


def setup_inputs(seed: int = 0) -> dict:
    arg_keys = jax.random.split(jax.random.key(seed), 7)
    return {
        "solution": bell_draw(arg_keys[0], (P_SIZE, NX, NY, NZ), 0.2, 1.2, ((0, 16), (1, 16)), jnp.float32),
        "source": bell_draw(arg_keys[1], (P_SIZE, NX, NY, NZ), 1.0, 6.0, ((0, 16), (1, 16)), jnp.float32),
        "mean_conductivity": jnp.clip(0.5 + 1.5 * jax.random.uniform(arg_keys[2], (NX, NY, NZ), jnp.float32) ** steps_of(arg_keys[2], (NX, NY, NZ), ((0, 16),), -0.2, 0.2), 0.5, 2.0),
        "kl_fields": bell_draw(arg_keys[3], (KL, NX, NY, NZ), 0.15, 0.9, ((1, 16),), jnp.float32),
        "couplings": draw_couplings(jax.random.fold_in(arg_keys[6], 71), 0),
        "mode_index": draw_mode_index(jax.random.fold_in(arg_keys[6], 71), 0),
    }


def periodic_pad(values, which_dim):
    length = values.shape[which_dim]
    last = lax.slice_in_dim(values, length - 1, length, axis=which_dim)
    first = lax.slice_in_dim(values, 0, 1, axis=which_dim)
    return jnp.concatenate([last, values, first], axis=which_dim)

def diffuse(coefficient, padded):
    center = coefficient[1:-1]
    values = padded[..., 1:-1, :, :]
    total = 0.5 * (center + coefficient[2:]) * (values - padded[..., 2:, :, :])
    total = total + 0.5 * (center + coefficient[:-2]) * (values - padded[..., :-2, :, :])
    for which_dim in (-2, -1):
        for offset in (-1, 1):
            total = total + 0.5 * (center + jnp.roll(center, offset, which_dim)) * (values - jnp.roll(values, offset, which_dim))
    return total

def reference(solution, source, mean_conductivity, kl_fields, couplings, mode_index):
    padded_solution = periodic_pad(solution, 1)
    mean_pad = periodic_pad(mean_conductivity, 0)
    kl_pad = periodic_pad(kl_fields, 1)
    mode_ids = jnp.arange(P_SIZE, dtype=jnp.int32)
    image = solution + diffuse(mean_pad, padded_solution)
    for field_id in range(KL):
        applied = diffuse(kl_pad[field_id], padded_solution)
        partners = couplings[field_id]
        degree = mode_index[:, field_id]
        for second in range(S):
            column = partners[:, second]
            strength = jnp.sqrt(jnp.maximum(degree, degree[column]).astype(jnp.float32))
            weight = jnp.where(column != mode_ids, strength, jnp.zeros_like(strength))
            image = image + weight[:, None, None, None] * applied[column]
    residual = source - image
    theta = 13.0
    delta = 12.0
    sigma = theta / delta
    rho = 1.0 / sigma
    direction = residual / theta
    correction = direction
    remain = residual
    for step in range(STEPS):
        applied = direction + diffuse(mean_pad, periodic_pad(direction, 1))
        remain = remain - applied
        rho_next = 1.0 / (2.0 * sigma - rho)
        direction = rho_next * rho * direction + 2.0 * rho_next / delta * remain
        correction = correction + direction
        rho = rho_next
    return (residual, correction)
```

```python
import jax
import jax.numpy as jnp
from jax import lax
from jax.experimental import pallas as pl
from jax.experimental.pallas import tpu as pltpu
from jax.sharding import PartitionSpec as P

STEPS = 3
VMEM = pltpu.VMEM
SMEM = pltpu.SMEM


def ahead(a, axis):
    return pltpu.roll(a, a.shape[axis] - 1, axis)


def behind(a, axis):
    return pltpu.roll(a, 1, axis)


def mix_kernel(index, near_weight, far_weight, near, far, sol, src, mid, up, down, out, faces):
    fields = mid.shape[0]
    modes = sol.shape[0]
    for q in range(fields):
        center = mid[q]
        faces[q, 0] = 0.5 * (center + up[q])
        faces[q, 1] = 0.5 * (center + down[q])
        for d, axis in ((2, 0), (4, 1)):
            face = 0.5 * (center + ahead(center, axis))
            faces[q, d] = face
            faces[q, d + 1] = behind(face, axis)

    @pl.loop(0, modes)
    def _(i):
        value = sol[i]
        sums = [faces[0, d] * value for d in range(6)]
        for k in range(fields - 1):
            mixed = None
            for s in range(2):
                at = (k * modes + i) * 2 + s
                j = index[at]
                term = near_weight[at] * near[j] + far_weight[at] * far[j]
                mixed = term if mixed is None else mixed + term
            sums = [sums[d] + faces[k + 1, d] * mixed for d in range(6)]
        image = value
        for d, axis in ((2, 0), (4, 1)):
            flux = sums[d] - ahead(sums[d + 1], axis)
            image = image + (flux - behind(flux, axis))
        out[i, 0] = src[i] - image
        out[i, 1] = sums[0]
        out[i, 2] = sums[1]
        out[i, 3] = mid[0]


def cheb_kernel(got, out, faces, direction, remain):
    planes = got.shape[0]
    for x in range(planes):
        center = got[x, 3]
        faces[x, 0] = 0.5 * (center + got[(x + 1) % planes, 3])
        faces[x, 1] = 0.5 * (center + ahead(center, 0))
        faces[x, 2] = 0.5 * (center + ahead(center, 1))
    theta = 13.0
    delta = 12.0
    sigma = theta / delta
    rho = 1.0 / sigma
    for x in range(planes):
        before, after = (x - 1) % planes, (x + 1) % planes
        image = (got[x, 1] - got[after, 2]) + (got[x, 2] - got[before, 1])
        residual = got[x, 0] - image
        first = residual * (1.0 / theta)
        out[x, 0] = residual
        out[x, 1] = first
        remain[x] = residual
        direction[0, x] = first
    for step in range(STEPS):
        now, later = step % 2, (step + 1) % 2
        rho_next = 1.0 / (2.0 * sigma - rho)
        flux_x = faces[planes - 1, 0] * (direction[now, planes - 1] - direction[now, 0])
        for x in range(planes):
            value = direction[now, x]
            flux_next = faces[x, 0] * (value - direction[now, (x + 1) % planes])
            applied = value + (flux_next - flux_x)
            flux_x = flux_next
            for axis in (0, 1):
                flux = faces[x, axis + 1] * (value - ahead(value, axis))
                applied = applied + (flux - behind(flux, axis))
            left = remain[x] - applied
            remain[x] = left
            new = (rho_next * rho) * value + (2.0 * rho_next / delta) * left
            direction[later, x] = new
            out[x, 1] = out[x, 1] + new
        rho = rho_next


def whole(memory):
    return pl.BlockSpec(memory_space=memory)


def shards(solution, source, mean_conductivity, kl_fields, couplings, mode_index):
    modes, _, ny, nz = solution.shape
    planes = lax.axis_size("gx")
    blocks = lax.axis_size("ma")
    chips = blocks // 2
    block = lax.axis_index("ma")
    core = block % 2
    sol = solution[:, 0]
    src = source[:, 0]
    mid = jnp.concatenate([mean_conductivity, kl_fields[:, 0]], 0)
    fields = mid.shape[0]

    ring = [(i, (i + 1) % planes) for i in range(planes)]
    down = lax.ppermute(mid, "gx", ring)
    up = lax.ppermute(mid, "gx", [(j, i) for i, j in ring])

    same_core = [[2 * chip + c for chip in range(chips)] for c in range(2)]
    spread = jnp.broadcast_to(sol[None], (chips,) + sol.shape)
    near = lax.all_to_all(spread, "ma", 0, 0, tiled=True, axis_index_groups=same_core)
    far = lax.ppermute(near, "ma", [(i, i ^ 1) for i in range(blocks)])

    rows = lax.dynamic_slice_in_dim(couplings, block * modes, modes, 1)
    own = block * modes + lax.broadcasted_iota(jnp.int32, rows.shape, 1)
    degree = lax.dynamic_slice_in_dim(mode_index, block * modes, modes, 0).T
    higher = degree[:, :, None] + (1 - lax.broadcasted_iota(jnp.int32, rows.shape, 2))
    weight = jnp.where(rows != own, jnp.sqrt(higher.astype(jnp.float32)), 0.0)
    owner = rows // modes
    is_near = (owner % 2) == core
    index = ((owner // 2) * modes + rows % modes).reshape(-1)
    near_weight = jnp.where(is_near, weight, 0.0).reshape(-1)
    far_weight = jnp.where(is_near, 0.0, weight).reshape(-1)

    tile = (ny, nz)
    mixed = pl.pallas_call(
        mix_kernel,
        out_shape=jax.ShapeDtypeStruct((modes, 4) + tile, jnp.float32),
        in_specs=[whole(SMEM)] * 3 + [whole(VMEM)] * 7,
        out_specs=whole(VMEM),
        scratch_shapes=[VMEM((fields, 6) + tile, jnp.float32)],
        name="mix",
    )(
        index, near_weight, far_weight,
        near.reshape((chips * modes,) + tile), far.reshape((chips * modes,) + tile),
        sol, src, mid, up, down,
    )
    got = lax.all_to_all(mixed, "gx", 0, 0, tiled=True)
    done = pl.pallas_call(
        cheb_kernel,
        out_shape=jax.ShapeDtypeStruct((planes, 2) + tile, jnp.float32),
        in_specs=[whole(VMEM)],
        out_specs=whole(VMEM),
        scratch_shapes=[
            VMEM((planes, 3) + tile, jnp.float32),
            VMEM((2, planes) + tile, jnp.float32),
            VMEM((planes,) + tile, jnp.float32),
        ],
        name="cheb",
    )(got)
    back = lax.all_to_all(done, "gx", 0, 0, tiled=True)
    return (back[:, 0:1], back[:, 1:2])


def solution(mesh):
    in_specs = (
        P("ma", "gx", None, None),
        P("ma", "gx", None, None),
        P("gx", None, None),
        P(None, "gx", None, None),
        P(),
        P(),
    )
    out_specs = (P("ma", "gx", None, None), P("ma", "gx", None, None))
    return jax.shard_map(shards, mesh=mesh, in_specs=in_specs, out_specs=out_specs, check_vma=False)
```

```python
import jax
import jax.numpy as jnp
from jax import lax
from jax.experimental import pallas as pl
from jax.experimental.pallas import tpu as pltpu
from jax.sharding import PartitionSpec as P

STEPS = 3
VMEM = pltpu.VMEM
SMEM = pltpu.SMEM


def ahead(a, axis):
    return pltpu.roll(a, a.shape[axis] - 1, axis)


def behind(a, axis):
    return pltpu.roll(a, 1, axis)


def mixture(index, weight, modes_in, k, i):
    mixed = None
    for s in range(2):
        at = 2 * k + s
        term = weight[at, i] * modes_in[index[at, i]]
        mixed = term if mixed is None else mixed + term
    return mixed


def near_kernel(index, weight, near, sol, mid, up, down, sums, faces):
    fields = mid.shape[0]
    for q in range(fields):
        center = mid[q]
        faces[q, 0] = 0.5 * (center + up[q])
        faces[q, 1] = 0.5 * (center + down[q])
        for d, axis in ((2, 0), (4, 1)):
            face = 0.5 * (center + ahead(center, axis))
            faces[q, d] = face
            faces[q, d + 1] = behind(face, axis)

    @pl.loop(0, sol.shape[0])
    def _(i):
        value = sol[i]
        parts = [faces[0, d] * value for d in range(6)]
        for k in range(fields - 1):
            mixed = mixture(index, weight, near, k, i)
            parts = [parts[d] + faces[k + 1, d] * mixed for d in range(6)]
        for d in range(6):
            sums[i, d] = parts[d]


def far_kernel(index, weight, far, sol, src, mid, sums, faces, out):
    @pl.loop(0, sol.shape[0])
    def _(i):
        parts = [sums[i, d] for d in range(6)]
        for k in range(faces.shape[0] - 1):
            mixed = mixture(index, weight, far, k, i)
            parts = [parts[d] + faces[k + 1, d] * mixed for d in range(6)]
        image = sol[i]
        for d, axis in ((2, 0), (4, 1)):
            flux = parts[d] - ahead(parts[d + 1], axis)
            image = image + (flux - behind(flux, axis))
        out[i, 0] = src[i] - image
        out[i, 1] = parts[0]
        out[i, 2] = parts[1]
        out[i, 3] = mid[0]


def cheb_kernel(got, out, faces, direction, remain):
    planes = got.shape[0]
    for x in range(planes):
        center = got[x, 3]
        faces[x, 0] = 0.5 * (center + got[(x + 1) % planes, 3])
        faces[x, 1] = 0.5 * (center + ahead(center, 0))
        faces[x, 2] = 0.5 * (center + ahead(center, 1))
    theta = 13.0
    delta = 12.0
    sigma = theta / delta
    rho = 1.0 / sigma
    for x in range(planes):
        before, after = (x - 1) % planes, (x + 1) % planes
        image = (got[x, 1] - got[after, 2]) + (got[x, 2] - got[before, 1])
        residual = got[x, 0] - image
        first = residual * (1.0 / theta)
        out[x, 0] = residual
        out[x, 1] = first
        remain[x] = residual
        direction[0, x] = first
    for step in range(STEPS):
        now, later = step % 2, (step + 1) % 2
        rho_next = 1.0 / (2.0 * sigma - rho)
        flux_x = faces[planes - 1, 0] * (direction[now, planes - 1] - direction[now, 0])
        for x in range(planes):
            value = direction[now, x]
            flux_next = faces[x, 0] * (value - direction[now, (x + 1) % planes])
            applied = value + (flux_next - flux_x)
            flux_x = flux_next
            for axis in (0, 1):
                flux = faces[x, axis + 1] * (value - ahead(value, axis))
                applied = applied + (flux - behind(flux, axis))
            left = remain[x] - applied
            remain[x] = left
            new = (rho_next * rho) * value + (2.0 * rho_next / delta) * left
            direction[later, x] = new
            out[x, 1] = out[x, 1] + new
        rho = rho_next


def whole(memory):
    return pl.BlockSpec(memory_space=memory)


def kernel_of(body, outs, memories, scratch=(), flops=0, size=0):
    return pl.pallas_call(
        body,
        out_shape=outs,
        in_specs=[whole(m) for m in memories],
        out_specs=jax.tree.map(lambda _: whole(VMEM), outs),
        scratch_shapes=list(scratch),
        compiler_params=pltpu.CompilerParams(vmem_limit_bytes=8 << 20),
        cost_estimate=pl.CostEstimate(flops=flops, bytes_accessed=size, transcendentals=0),
    )


def f32(*shape):
    return jax.ShapeDtypeStruct(shape, jnp.float32)


def step(solution, source, mean_conductivity, kl_fields, couplings, mode_index):
    modes, _, ny, nz = solution.shape
    planes = lax.axis_size("gx")
    blocks = lax.axis_size("ma")
    chips = blocks // 2
    block = lax.axis_index("ma")
    core = block % 2
    sol = solution[:, 0]
    src = source[:, 0]
    mid = jnp.concatenate([mean_conductivity, kl_fields[:, 0]], 0)
    fields = mid.shape[0]

    ring = [(i, (i + 1) % planes) for i in range(planes)]
    down = lax.ppermute(mid, "gx", ring)
    up = lax.ppermute(mid, "gx", [(j, i) for i, j in ring])

    same_core = [[2 * chip + c for chip in range(chips)] for c in range(2)]
    spread = jnp.broadcast_to(sol[None], (chips,) + sol.shape)
    near = lax.all_to_all(spread, "ma", 0, 0, tiled=True, axis_index_groups=same_core)
    far = lax.ppermute(near, "ma", [(i, i ^ 1) for i in range(blocks)])

    rows = lax.dynamic_slice_in_dim(couplings, block * modes, modes, 1).transpose(0, 2, 1)
    own = block * modes + lax.broadcasted_iota(jnp.int32, rows.shape, 2)
    degree = lax.dynamic_slice_in_dim(mode_index, block * modes, modes, 0).T
    higher = degree[:, None, :] + (1 - lax.broadcasted_iota(jnp.int32, rows.shape, 1))
    weight = jnp.where(rows != own, jnp.sqrt(higher.astype(jnp.float32)), 0.0)
    owner = rows >> (modes.bit_length() - 1)
    is_near = (owner & 1) == core
    flat = (2 * (fields - 1), modes)
    index = ((owner >> 1) * modes + (rows & (modes - 1))).reshape(flat)
    near_weight = jnp.where(is_near, weight, 0.0).reshape(flat)
    far_weight = jnp.where(is_near, 0.0, weight).reshape(flat)

    tile = (ny, nz)
    cell = ny * nz
    pool = (chips * modes,) + tile
    sums, faces = kernel_of(
        near_kernel, (f32(modes, 6, *tile), f32(fields, 6, *tile)), [SMEM] * 2 + [VMEM] * 5,
        flops=modes * fields * 16 * cell, size=4 * cell * (chips * modes + 8 * modes + 9 * fields),
    )(index, near_weight, near.reshape(pool), sol, mid, up, down)
    mixed = kernel_of(
        far_kernel, f32(modes, 4, *tile), [SMEM] * 2 + [VMEM] * 6,
        flops=modes * fields * 16 * cell, size=4 * cell * (chips * modes + 12 * modes + 7 * fields),
    )(index, far_weight, far.reshape(pool), sol, src, mid, sums, faces)
    got = lax.all_to_all(mixed, "gx", 0, 0, tiled=True)
    done = kernel_of(
        cheb_kernel, f32(planes, 2, *tile), [VMEM],
        [VMEM((planes, 3) + tile, jnp.float32), VMEM((2, planes) + tile, jnp.float32), VMEM((planes,) + tile, jnp.float32)],
        flops=planes * STEPS * 30 * cell, size=4 * cell * planes * 6,
    )(got)
    back = lax.all_to_all(done, "gx", 0, 0, tiled=True)
    return (back[:, 0:1], back[:, 1:2])


def solution(mesh):
    in_specs = (
        P("ma", "gx", None, None),
        P("ma", "gx", None, None),
        P("gx", None, None),
        P(None, "gx", None, None),
        P(),
        P(),
    )
    out_specs = (P("ma", "gx", None, None), P("ma", "gx", None, None))
    return jax.shard_map(step, mesh=mesh, in_specs=in_specs, out_specs=out_specs, check_vma=False)
```

```python
import jax
import jax.numpy as jnp
from jax import lax
from jax.experimental import pallas as pl
from jax.experimental.pallas import tpu as pltpu
from jax.sharding import PartitionSpec as P

STEPS = 3
VMEM = pltpu.VMEM
SMEM = pltpu.SMEM


def ahead(a, axis):
    return pltpu.roll(a, a.shape[axis] - 1, axis)


def behind(a, axis):
    return pltpu.roll(a, 1, axis)


def mixture(index, weight, modes_in, k, i):
    mixed = None
    for s in range(2):
        at = 2 * k + s
        term = weight[at, i] * modes_in[index[at, i]]
        mixed = term if mixed is None else mixed + term
    return mixed


def face_kernel(mid, up, down, faces):
    for q in range(mid.shape[0]):
        center = mid[q]
        faces[q, 0] = 0.5 * (center + up[q])
        faces[q, 1] = 0.5 * (center + down[q])
        for d, axis in ((2, 0), (4, 1)):
            face = 0.5 * (center + ahead(center, axis))
            faces[q, d] = face
            faces[q, d + 1] = behind(face, axis)


def near_kernel(index, weight, near, sol, faces, sums):
    @pl.loop(0, sol.shape[0], unroll=2)
    def _(i):
        value = sol[i]
        parts = [faces[0, d] * value for d in range(6)]
        for k in range(faces.shape[0] - 1):
            mixed = mixture(index, weight, near, k, i)
            parts = [parts[d] + faces[k + 1, d] * mixed for d in range(6)]
        for d in range(6):
            sums[i, d] = parts[d]


def far_kernel(index, weight, far, sol, src, sums, faces, out):
    @pl.loop(0, sol.shape[0], unroll=4)
    def _(i):
        parts = [sums[i, d] for d in range(6)]
        for k in range(faces.shape[0] - 1):
            mixed = mixture(index, weight, far, k, i)
            parts = [parts[d] + faces[k + 1, d] * mixed for d in range(6)]
        image = sol[i]
        for d, axis in ((2, 0), (4, 1)):
            flux = parts[d] - ahead(parts[d + 1], axis)
            image = image + (flux - behind(flux, axis))
        out[i, 0] = src[i] - image
        out[i, 1] = parts[0]
        out[i, 2] = parts[1]


def cheb_kernel(place, got, near_mean, far_mean, out, mean, faces, direction, remain):
    planes = got.shape[0]
    split = near_mean.shape[0]
    for x in range(planes):
        mean[place[x]] = near_mean[x] if x < split else far_mean[x - split]
    center = mean[0]
    for x in range(planes):
        after = mean[(x + 1) % planes]
        faces[x, 0] = 0.5 * (center + after)
        faces[x, 1] = 0.5 * (center + ahead(center, 0))
        faces[x, 2] = 0.5 * (center + ahead(center, 1))
        center = after
    theta = 13.0
    delta = 12.0
    sigma = theta / delta
    rho = 1.0 / sigma
    for x in range(planes):
        before, after = (x - 1) % planes, (x + 1) % planes
        image = (got[x, 1] - got[after, 2]) + (got[x, 2] - got[before, 1])
        residual = got[x, 0] - image
        first = residual * (1.0 / theta)
        out[x, 0] = residual
        out[x, 1] = first
        remain[x] = residual
        direction[0, x] = first
    for step in range(STEPS):
        now, later = step % 2, (step + 1) % 2
        rho_next = 1.0 / (2.0 * sigma - rho)
        flux_x = faces[planes - 1, 0] * (direction[now, planes - 1] - direction[now, 0])
        for x in range(planes):
            value = direction[now, x]
            flux_next = faces[x, 0] * (value - direction[now, (x + 1) % planes])
            applied = value + (flux_next - flux_x)
            flux_x = flux_next
            for axis in (0, 1):
                flux = faces[x, axis + 1] * (value - ahead(value, axis))
                applied = applied + (flux - behind(flux, axis))
            left = remain[x] - applied
            remain[x] = left
            new = (rho_next * rho) * value + (2.0 * rho_next / delta) * left
            direction[later, x] = new
            out[x, 1] = out[x, 1] + new
        rho = rho_next


def whole(memory):
    return pl.BlockSpec(memory_space=memory)


def kernel_of(body, outs, memories, scratch=(), flops=0, size=0):
    return pl.pallas_call(
        body,
        out_shape=outs,
        in_specs=[whole(m) for m in memories],
        out_specs=jax.tree.map(lambda _: whole(VMEM), outs),
        scratch_shapes=list(scratch),
        compiler_params=pltpu.CompilerParams(vmem_limit_bytes=8 << 20),
        cost_estimate=pl.CostEstimate(flops=flops, bytes_accessed=size, transcendentals=0),
    )


def f32(*shape):
    return jax.ShapeDtypeStruct(shape, jnp.float32)


def step(solution, source, mean_conductivity, kl_fields, couplings, mode_index):
    modes, _, ny, nz = solution.shape
    planes = lax.axis_size("gx")
    blocks = lax.axis_size("ma")
    chips = blocks // 2
    block = lax.axis_index("ma")
    core = block % 2
    sol = solution[:, 0]
    src = source[:, 0]
    mid = jnp.concatenate([mean_conductivity, kl_fields[:, 0]], 0)
    fields = mid.shape[0]

    def shifted(array, hops):
        return lax.ppermute(array, "gx", [(i, (i + hops) % planes) for i in range(planes)])

    down = shifted(mid, 1)
    up = shifted(mid, -1)

    same_core = [[2 * chip + c for chip in range(chips)] for c in range(2)]
    spread = jnp.broadcast_to(sol[None], (chips,) + sol.shape)
    near = lax.all_to_all(spread, "ma", 0, 0, tiled=True, axis_index_groups=same_core)
    far = lax.ppermute(near, "ma", [(i, i ^ 1) for i in range(blocks)])

    rows = lax.dynamic_slice_in_dim(couplings, block * modes, modes, 1).transpose(0, 2, 1)
    own = block * modes + lax.broadcasted_iota(jnp.int32, rows.shape, 2)
    degree = lax.dynamic_slice_in_dim(mode_index, block * modes, modes, 0).T
    higher = degree[:, None, :] + (1 - lax.broadcasted_iota(jnp.int32, rows.shape, 1))
    weight = jnp.where(rows != own, jnp.sqrt(higher.astype(jnp.float32)), 0.0)
    owner = rows >> (modes.bit_length() - 1)
    is_near = (owner & 1) == core
    flat = (2 * (fields - 1), modes)
    index = ((owner >> 1) * modes + (rows & (modes - 1))).reshape(flat)
    near_weight = jnp.where(is_near, weight, 0.0).reshape(flat)
    far_weight = jnp.where(is_near, 0.0, weight).reshape(flat)

    tile = (ny, nz)
    cell = ny * nz
    pool = (chips * modes,) + tile
    faces = kernel_of(
        face_kernel, f32(fields, 6, *tile), [VMEM] * 3, flops=fields * 10 * cell, size=4 * cell * 9 * fields
    )(mid, up, down)
    sums = kernel_of(
        near_kernel, f32(modes, 6, *tile), [SMEM] * 2 + [VMEM] * 3,
        flops=modes * fields * 16 * cell, size=4 * cell * (chips * modes + 8 * modes + 6 * fields),
    )(index, near_weight, near.reshape(pool), sol, faces)
    mixed = kernel_of(
        far_kernel, f32(modes, 3, *tile), [SMEM] * 2 + [VMEM] * 5,
        flops=modes * fields * 16 * cell, size=4 * cell * (chips * modes + 11 * modes + 6 * fields),
    )(index, far_weight, far.reshape(pool), sol, src, sums, faces)
    three = jnp.concatenate([down[:1], mid[:1], up[:1]], 0)
    low = shifted(three, 3)
    high = shifted(three, -3)
    nine = jnp.concatenate([low, three, high], 0)
    rest = shifted(nine[1:8], planes // 2)
    place = lax.rem(lax.iota(jnp.int32, planes) + (lax.axis_index("gx") + planes - 4), planes)
    got = lax.all_to_all(mixed, "gx", 0, 0, tiled=True)
    done = kernel_of(
        cheb_kernel, f32(planes, 2, *tile), [SMEM] + [VMEM] * 3,
        [VMEM((planes,) + tile, jnp.float32), VMEM((planes, 3) + tile, jnp.float32), VMEM((2, planes) + tile, jnp.float32), VMEM((planes,) + tile, jnp.float32)],
        flops=planes * STEPS * 30 * cell, size=4 * cell * planes * 6,
    )(place, got, nine, rest)
    back = lax.all_to_all(done, "gx", 0, 0, tiled=True)
    return (back[:, 0:1], back[:, 1:2])


def solution(mesh):
    in_specs = (
        P("ma", "gx", None, None),
        P("ma", "gx", None, None),
        P("gx", None, None),
        P(None, "gx", None, None),
        P(),
        P(),
    )
    out_specs = (P("ma", "gx", None, None), P("ma", "gx", None, None))
    return jax.shard_map(step, mesh=mesh, in_specs=in_specs, out_specs=out_specs, check_vma=False)
```

```python
import jax
import jax.numpy as jnp
from jax import lax
from jax.experimental import pallas as pl
from jax.experimental.pallas import tpu as pltpu
from jax.sharding import PartitionSpec as P

STEPS = 3
VMEM = pltpu.VMEM
SMEM = pltpu.SMEM


def ahead(a, axis):
    return pltpu.roll(a, a.shape[axis] - 1, axis)


def behind(a, axis):
    return pltpu.roll(a, 1, axis)


def mixture(index, weight, modes_in, k, i):
    mixed = None
    for s in range(2):
        at = 2 * k + s
        term = weight[at, i] * modes_in[index[at, i]]
        mixed = term if mixed is None else mixed + term
    return mixed


def face_kernel(mid, mine, theirs, faces):
    first = lax.rem(lax.axis_index("ma"), 2) == 0
    for q in range(mid.shape[0]):
        center = mid[q]
        faces[q, 0] = 0.5 * (center + jnp.where(first, theirs[q], mine[q]))
        faces[q, 1] = 0.5 * (center + jnp.where(first, mine[q], theirs[q]))
        for d, axis in ((2, 0), (4, 1)):
            face = 0.5 * (center + ahead(center, axis))
            faces[q, d] = face
            faces[q, d + 1] = behind(face, axis)


def near_kernel(index, weight, near, sol, faces, sums):
    @pl.loop(0, sol.shape[0], unroll=2)
    def _(i):
        value = sol[i]
        parts = [faces[0, d] * value for d in range(6)]
        for k in range(faces.shape[0] - 1):
            mixed = mixture(index, weight, near, k, i)
            parts = [parts[d] + faces[k + 1, d] * mixed for d in range(6)]
        for d in range(6):
            sums[i, d] = parts[d]


def far_kernel(index, weight, far, sol, src, sums, faces, out):
    @pl.loop(0, sol.shape[0], unroll=4)
    def _(i):
        parts = [sums[i, d] for d in range(6)]
        for k in range(faces.shape[0] - 1):
            mixed = mixture(index, weight, far, k, i)
            parts = [parts[d] + faces[k + 1, d] * mixed for d in range(6)]
        image = sol[i]
        for d, axis in ((2, 0), (4, 1)):
            flux = parts[d] - ahead(parts[d + 1], axis)
            image = image + (flux - behind(flux, axis))
        out[i, 0] = src[i] - image
        out[i, 1] = parts[0]
        out[i, 2] = parts[1]


def cheb_kernel(got, near_mean, far_mean, out, mean, faces, direction, remain):
    planes = got.shape[0]
    split = near_mean.shape[0]
    first = lax.axis_index("gx") + planes - 4
    for x in range(planes):
        mean[lax.rem(first + x, planes)] = near_mean[x] if x < split else far_mean[x - split]
    center = mean[0]
    for x in range(planes):
        after = mean[(x + 1) % planes]
        faces[x, 0] = 0.5 * (center + after)
        faces[x, 1] = 0.5 * (center + ahead(center, 0))
        faces[x, 2] = 0.5 * (center + ahead(center, 1))
        center = after
    theta = 13.0
    delta = 12.0
    sigma = theta / delta
    rho = 1.0 / sigma
    for x in range(planes):
        before, after = (x - 1) % planes, (x + 1) % planes
        image = (got[x, 1] - got[after, 2]) + (got[x, 2] - got[before, 1])
        residual = got[x, 0] - image
        first = residual * (1.0 / theta)
        out[x, 0] = residual
        out[x, 1] = first
        remain[x] = residual
        direction[0, x] = first
    for step in range(STEPS):
        now, later = step % 2, (step + 1) % 2
        rho_next = 1.0 / (2.0 * sigma - rho)
        flux_x = faces[planes - 1, 0] * (direction[now, planes - 1] - direction[now, 0])
        for x in range(planes):
            value = direction[now, x]
            flux_next = faces[x, 0] * (value - direction[now, (x + 1) % planes])
            applied = value + (flux_next - flux_x)
            flux_x = flux_next
            for axis in (0, 1):
                flux = faces[x, axis + 1] * (value - ahead(value, axis))
                applied = applied + (flux - behind(flux, axis))
            left = remain[x] - applied
            remain[x] = left
            new = (rho_next * rho) * value + (2.0 * rho_next / delta) * left
            direction[later, x] = new
            out[x, 1] = out[x, 1] + new
        rho = rho_next


def whole(memory):
    return pl.BlockSpec(memory_space=memory)


def kernel_of(body, outs, memories, scratch=(), flops=0, size=0):
    return pl.pallas_call(
        body,
        out_shape=outs,
        in_specs=[whole(m) for m in memories],
        out_specs=jax.tree.map(lambda _: whole(VMEM), outs),
        scratch_shapes=list(scratch),
        compiler_params=pltpu.CompilerParams(vmem_limit_bytes=8 << 20),
        cost_estimate=pl.CostEstimate(flops=flops, bytes_accessed=size, transcendentals=0),
    )


def f32(*shape):
    return jax.ShapeDtypeStruct(shape, jnp.float32)


def step(solution, source, mean_conductivity, kl_fields, couplings, mode_index):
    modes, _, ny, nz = solution.shape
    planes = lax.axis_size("gx")
    blocks = lax.axis_size("ma")
    chips = blocks // 2
    block = lax.axis_index("ma")
    core = block % 2
    sol = solution[:, 0]
    src = source[:, 0]
    mid = jnp.concatenate([mean_conductivity, kl_fields[:, 0]], 0)
    fields = mid.shape[0]

    def shifted(array, hops):
        pairs = []
        for x in range(planes):
            for y in range(blocks):
                target = (x + (hops if y % 2 == 0 else -hops)) % planes
                pairs.append((x * blocks + y, target * blocks + y))
        return lax.ppermute(array, ("gx", "ma"), pairs)

    def swapped(array):
        return lax.ppermute(array, "ma", [(i, i ^ 1) for i in range(blocks)])

    def ordered(mine, theirs):
        return jnp.where(core == 0, mine, theirs), jnp.where(core == 0, theirs, mine)

    mine = shifted(mid, 1)
    theirs = swapped(mine)

    same_core = [[2 * chip + c for chip in range(chips)] for c in range(2)]
    spread = jnp.broadcast_to(sol[None], (chips,) + sol.shape)
    near = lax.all_to_all(spread, "ma", 0, 0, tiled=True, axis_index_groups=same_core)
    far = swapped(near)

    rows = lax.dynamic_slice_in_dim(couplings, block * modes, modes, 1).transpose(0, 2, 1)
    own = block * modes + lax.broadcasted_iota(jnp.int32, rows.shape, 2)
    degree = lax.dynamic_slice_in_dim(mode_index, block * modes, modes, 0).T
    higher = degree[:, None, :] + (1 - lax.broadcasted_iota(jnp.int32, rows.shape, 1))
    weight = jnp.where(rows != own, jnp.sqrt(higher.astype(jnp.float32)), 0.0)
    owner = rows >> (modes.bit_length() - 1)
    is_near = (owner & 1) == core
    flat = (2 * (fields - 1), modes)
    index = ((owner >> 1) * modes + (rows & (modes - 1))).reshape(flat)
    near_weight = jnp.where(is_near, weight, 0.0).reshape(flat)
    far_weight = jnp.where(is_near, 0.0, weight).reshape(flat)

    tile = (ny, nz)
    cell = ny * nz
    pool = (chips * modes,) + tile
    faces = kernel_of(
        face_kernel, f32(fields, 6, *tile), [VMEM] * 3, flops=fields * 10 * cell, size=4 * cell * 9 * fields
    )(mid, mine, theirs)
    sums = kernel_of(
        near_kernel, f32(modes, 6, *tile), [SMEM] * 2 + [VMEM] * 3,
        flops=modes * fields * 16 * cell, size=4 * cell * (chips * modes + 8 * modes + 6 * fields),
    )(index, near_weight, near.reshape(pool), sol, faces)
    mixed = kernel_of(
        far_kernel, f32(modes, 3, *tile), [SMEM] * 2 + [VMEM] * 5,
        flops=modes * fields * 16 * cell, size=4 * cell * (chips * modes + 11 * modes + 6 * fields),
    )(index, far_weight, far.reshape(pool), sol, src, sums, faces)
    down, up = ordered(mine[:1], theirs[:1])
    three = jnp.concatenate([down, mid[:1], up], 0)
    mean_mine = shifted(three, 3)
    mean_theirs = swapped(mean_mine)
    low, high = ordered(mean_mine, mean_theirs)
    nine = jnp.concatenate([low, three, high], 0)
    rest = shifted(nine[1:8], planes // 2)
    got = lax.all_to_all(mixed, "gx", 0, 0, tiled=True)
    done = kernel_of(
        cheb_kernel, f32(planes, 2, *tile), [VMEM] * 3,
        [VMEM((planes,) + tile, jnp.float32), VMEM((planes, 3) + tile, jnp.float32), VMEM((2, planes) + tile, jnp.float32), VMEM((planes,) + tile, jnp.float32)],
        flops=planes * STEPS * 30 * cell, size=4 * cell * planes * 6,
    )(got, nine, rest)
    back = lax.all_to_all(done, "gx", 0, 0, tiled=True)
    return (back[:, 0:1], back[:, 1:2])


def solution(mesh):
    in_specs = (
        P("ma", "gx", None, None),
        P("ma", "gx", None, None),
        P("gx", None, None),
        P(None, "gx", None, None),
        P(),
        P(),
    )
    out_specs = (P("ma", "gx", None, None), P("ma", "gx", None, None))
    return jax.shard_map(step, mesh=mesh, in_specs=in_specs, out_specs=out_specs, check_vma=False)
```

```python
import jax
import jax.numpy as jnp
from jax import lax
from jax.experimental import pallas as pl
from jax.experimental.pallas import tpu as pltpu
from jax.sharding import PartitionSpec as P

STEPS = 3
VMEM = pltpu.VMEM
SMEM = pltpu.SMEM


def ahead(a, axis):
    return pltpu.roll(a, a.shape[axis] - 1, axis)


def behind(a, axis):
    return pltpu.roll(a, 1, axis)


def mixture(index, weight, modes_in, k, i):
    mixed = None
    for s in range(2):
        at = 2 * k + s
        term = weight[at, i] * modes_in[index[at, i]]
        mixed = term if mixed is None else mixed + term
    return mixed


def face_kernel(mid, mine, theirs, faces):
    first = lax.rem(lax.axis_index("ma"), 2) == 0
    for q in range(mid.shape[0]):
        center = mid[q]
        faces[q, 0] = 0.5 * (center + jnp.where(first, theirs[q], mine[q]))
        faces[q, 1] = 0.5 * (center + jnp.where(first, mine[q], theirs[q]))
        for d, axis in ((2, 0), (4, 1)):
            face = 0.5 * (center + ahead(center, axis))
            faces[q, d] = face
            faces[q, d + 1] = behind(face, axis)


def add_mixtures(index, weight, pool, faces, rows, parts):
    for k in range(faces.shape[0] - 1):
        mixed = [mixture(index, weight, pool, k, i) for i in rows]
        for d in range(6):
            face = faces[k + 1, d]
            for n in range(len(rows)):
                parts[n][d] = parts[n][d] + face * mixed[n]
    return parts


def near_kernel(index, weight, near, faces, sums):
    modes = sums.shape[0]
    first = lax.div(lax.axis_index("ma"), 2) * modes

    @pl.loop(0, modes // 2, unroll=8)
    def _(pair):
        rows = (2 * pair, 2 * pair + 1)
        values = [near[first + i] for i in rows]
        parts = [[faces[0, d] * value for d in range(6)] for value in values]
        parts = add_mixtures(index, weight, near, faces, rows, parts)
        for n, i in enumerate(rows):
            for d in range(6):
                sums[i, d] = parts[n][d]


def far_kernel(index, weight, far, sol, src, sums, faces, out):
    @pl.loop(0, sol.shape[0] // 2, unroll=8)
    def _(pair):
        rows = (2 * pair, 2 * pair + 1)
        parts = [[sums[i, d] for d in range(6)] for i in rows]
        parts = add_mixtures(index, weight, far, faces, rows, parts)
        for n, i in enumerate(rows):
            image = sol[i]
            for d, axis in ((2, 0), (4, 1)):
                flux = parts[n][d] - ahead(parts[n][d + 1], axis)
                image = image + (flux - behind(flux, axis))
            out[i, 0] = src[i] - image
            out[i, 1] = parts[n][0]
            out[i, 2] = parts[n][1]


def cheb_kernel(got, near_mean, far_mean, out, mean, faces, direction, remain):
    planes = got.shape[0]
    split = near_mean.shape[0]
    first = lax.axis_index("gx") + planes - 4
    for x in range(planes):
        mean[lax.rem(first + x, planes)] = near_mean[x] if x < split else far_mean[x - split]
    center = mean[0]
    for x in range(planes):
        after = mean[(x + 1) % planes]
        faces[x, 0] = 0.5 * (center + after)
        faces[x, 1] = 0.5 * (center + ahead(center, 0))
        faces[x, 2] = 0.5 * (center + ahead(center, 1))
        center = after
    theta = 13.0
    delta = 12.0
    sigma = theta / delta
    rho = 1.0 / sigma
    for x in range(planes):
        before, after = (x - 1) % planes, (x + 1) % planes
        image = (got[x, 1] - got[after, 2]) + (got[x, 2] - got[before, 1])
        residual = got[x, 0] - image
        first = residual * (1.0 / theta)
        out[x, 0] = residual
        out[x, 1] = first
        remain[x] = residual
        direction[0, x] = first
    for step in range(STEPS):
        now, later = step % 2, (step + 1) % 2
        rho_next = 1.0 / (2.0 * sigma - rho)
        flux_x = faces[planes - 1, 0] * (direction[now, planes - 1] - direction[now, 0])
        for x in range(planes):
            value = direction[now, x]
            flux_next = faces[x, 0] * (value - direction[now, (x + 1) % planes])
            applied = value + (flux_next - flux_x)
            flux_x = flux_next
            for axis in (0, 1):
                flux = faces[x, axis + 1] * (value - ahead(value, axis))
                applied = applied + (flux - behind(flux, axis))
            left = remain[x] - applied
            remain[x] = left
            new = (rho_next * rho) * value + (2.0 * rho_next / delta) * left
            direction[later, x] = new
            out[x, 1] = out[x, 1] + new
        rho = rho_next


def whole(memory):
    return pl.BlockSpec(memory_space=memory)


def kernel_of(body, outs, memories, scratch=(), flops=0, size=0):
    return pl.pallas_call(
        body,
        out_shape=outs,
        in_specs=[whole(m) for m in memories],
        out_specs=jax.tree.map(lambda _: whole(VMEM), outs),
        scratch_shapes=list(scratch),
        compiler_params=pltpu.CompilerParams(vmem_limit_bytes=8 << 20),
        cost_estimate=pl.CostEstimate(flops=flops, bytes_accessed=size, transcendentals=0),
    )


def f32(*shape):
    return jax.ShapeDtypeStruct(shape, jnp.float32)


def step(solution, source, mean_conductivity, kl_fields, couplings, mode_index):
    modes, _, ny, nz = solution.shape
    planes = lax.axis_size("gx")
    blocks = lax.axis_size("ma")
    chips = blocks // 2
    block = lax.axis_index("ma")
    core = block % 2
    sol = solution[:, 0]
    src = source[:, 0]
    mid = jnp.concatenate([mean_conductivity, kl_fields[:, 0]], 0)
    fields = mid.shape[0]

    def shifted(array, hops):
        pairs = []
        for x in range(planes):
            for y in range(blocks):
                target = (x + (hops if y % 2 == 0 else -hops)) % planes
                pairs.append((x * blocks + y, target * blocks + y))
        return lax.ppermute(array, ("gx", "ma"), pairs)

    def swapped(array):
        return lax.ppermute(array, "ma", [(i, i ^ 1) for i in range(blocks)])

    def ordered(mine, theirs):
        return jnp.where(core == 0, mine, theirs), jnp.where(core == 0, theirs, mine)

    mine = shifted(mid, 1)
    theirs = swapped(mine)

    same_core = [[2 * chip + c for chip in range(chips)] for c in range(2)]
    spread = jnp.broadcast_to(sol[None], (chips,) + sol.shape)
    near = lax.all_to_all(spread, "ma", 0, 0, tiled=True, axis_index_groups=same_core)
    far = swapped(near)

    rows = lax.dynamic_slice_in_dim(couplings, block * modes, modes, 1).transpose(0, 2, 1)
    own = block * modes + lax.broadcasted_iota(jnp.int32, rows.shape, 2)
    degree = lax.dynamic_slice_in_dim(mode_index, block * modes, modes, 0).T
    higher = degree[:, None, :] + (1 - lax.broadcasted_iota(jnp.int32, rows.shape, 1))
    weight = jnp.where(rows != own, jnp.sqrt(higher.astype(jnp.float32)), 0.0)
    owner = rows >> (modes.bit_length() - 1)
    is_near = (owner & 1) == core
    flat = (2 * (fields - 1), modes)
    index = ((owner >> 1) * modes + (rows & (modes - 1))).reshape(flat)
    near_weight = jnp.where(is_near, weight, 0.0).reshape(flat)
    far_weight = jnp.where(is_near, 0.0, weight).reshape(flat)

    tile = (ny, nz)
    cell = ny * nz
    pool = (chips * modes,) + tile
    faces = kernel_of(
        face_kernel, f32(fields, 6, *tile), [VMEM] * 3, flops=fields * 10 * cell, size=4 * cell * 9 * fields
    )(mid, mine, theirs)
    sums = kernel_of(
        near_kernel, f32(modes, 6, *tile), [SMEM] * 2 + [VMEM] * 2,
        flops=modes * fields * 16 * cell, size=4 * cell * (chips * modes + 8 * modes + 6 * fields),
    )(index, near_weight, near.reshape(pool), faces)
    mixed = kernel_of(
        far_kernel, f32(modes, 3, *tile), [SMEM] * 2 + [VMEM] * 5,
        flops=modes * fields * 16 * cell, size=4 * cell * (chips * modes + 11 * modes + 6 * fields),
    )(index, far_weight, far.reshape(pool), sol, src, sums, faces)
    down, up = ordered(mine[:1], theirs[:1])
    three = jnp.concatenate([down, mid[:1], up], 0)
    mean_mine = shifted(three, 3)
    mean_theirs = swapped(mean_mine)
    low, high = ordered(mean_mine, mean_theirs)
    nine = jnp.concatenate([low, three, high], 0)
    rest = shifted(nine[1:8], planes // 2)
    got = lax.all_to_all(mixed, "gx", 0, 0, tiled=True)
    done = kernel_of(
        cheb_kernel, f32(planes, 2, *tile), [VMEM] * 3,
        [VMEM((planes,) + tile, jnp.float32), VMEM((planes, 3) + tile, jnp.float32), VMEM((2, planes) + tile, jnp.float32), VMEM((planes,) + tile, jnp.float32)],
        flops=planes * STEPS * 30 * cell, size=4 * cell * planes * 6,
    )(got, nine, rest)
    back = lax.all_to_all(done, "gx", 0, 0, tiled=True)
    return (back[:, 0:1], back[:, 1:2])


def solution(mesh):
    in_specs = (
        P("ma", "gx", None, None),
        P("ma", "gx", None, None),
        P("gx", None, None),
        P(None, "gx", None, None),
        P(),
        P(),
    )
    out_specs = (P("ma", "gx", None, None), P("ma", "gx", None, None))
    return jax.shard_map(step, mesh=mesh, in_specs=in_specs, out_specs=out_specs, check_vma=False)
```

```python
import jax
import jax.numpy as jnp
from jax import lax
from jax.experimental import pallas as pl
from jax.experimental.pallas import tpu as pltpu
from jax.sharding import PartitionSpec as P

STEPS = 3
VMEM = pltpu.VMEM
SMEM = pltpu.SMEM


def ahead(a, axis):
    return pltpu.roll(a, a.shape[axis] - 1, axis)


def behind(a, axis):
    return pltpu.roll(a, 1, axis)


def mixture(index, weight, modes_in, k, i):
    mixed = None
    for s in range(2):
        at = 2 * k + s
        term = weight[at, i] * modes_in[index[at, i]]
        mixed = term if mixed is None else mixed + term
    return mixed


def face_kernel(mid, mine, theirs, faces):
    first = lax.rem(lax.axis_index("ma"), 2) == 0
    for q in range(mid.shape[0]):
        center = mid[q]
        faces[q, 0] = 0.5 * (center + jnp.where(first, theirs[q], mine[q]))
        faces[q, 1] = 0.5 * (center + jnp.where(first, mine[q], theirs[q]))
        for d, axis in ((2, 0), (4, 1)):
            face = 0.5 * (center + ahead(center, axis))
            faces[q, d] = face
            faces[q, d + 1] = behind(face, axis)


def add_mixtures(index, weight, pool, faces, rows, parts):
    for k in range(faces.shape[0] - 1):
        mixed = [mixture(index, weight, pool, k, i) for i in rows]
        for d in range(6):
            face = faces[k + 1, d]
            for n in range(len(rows)):
                parts[n][d] = parts[n][d] + face * mixed[n]
    return parts


def near_kernel(index, weight, near, faces, sums):
    modes = sums.shape[0]
    first = lax.div(lax.axis_index("ma"), 2) * modes

    @pl.loop(0, modes // 2, unroll=8)
    def _(pair):
        rows = (2 * pair, 2 * pair + 1)
        values = [near[first + i] for i in rows]
        parts = [[faces[0, d] * value for d in range(6)] for value in values]
        parts = add_mixtures(index, weight, near, faces, rows, parts)
        for n, i in enumerate(rows):
            for d in range(6):
                sums[i, d] = parts[n][d]


def far_kernel(index, weight, far, sol, src, sums, faces, out, held, sems):
    writes = []
    for pair in range(sol.shape[0] // 2):
        rows = (2 * pair, 2 * pair + 1)
        parts = [[sums[i, d] for d in range(6)] for i in rows]
        parts = add_mixtures(index, weight, far, faces, rows, parts)
        for n, i in enumerate(rows):
            image = sol[i]
            for d, axis in ((2, 0), (4, 1)):
                flux = parts[n][d] - ahead(parts[n][d + 1], axis)
                image = image + (flux - behind(flux, axis))
            held[i, 0] = src[i] - image
            held[i, 1] = parts[n][0]
            held[i, 2] = parts[n][1]
        slab = pl.ds(2 * pair, 2)
        writes.append(pltpu.make_async_copy(held.at[slab], out.at[slab], sems.at[pair]))
        writes[-1].start()
    for write in writes:
        write.wait()


def cheb_kernel(got, near_mean, far_mean, out, mean, faces, direction, remain):
    planes = got.shape[0]
    split = near_mean.shape[0]
    first = lax.axis_index("gx") + planes - 4
    for x in range(planes):
        mean[lax.rem(first + x, planes)] = near_mean[x] if x < split else far_mean[x - split]
    center = mean[0]
    for x in range(planes):
        after = mean[(x + 1) % planes]
        faces[x, 0] = 0.5 * (center + after)
        faces[x, 1] = 0.5 * (center + ahead(center, 0))
        faces[x, 2] = 0.5 * (center + ahead(center, 1))
        center = after
    theta = 13.0
    delta = 12.0
    sigma = theta / delta
    rho = 1.0 / sigma
    for x in range(planes):
        before, after = (x - 1) % planes, (x + 1) % planes
        image = (got[x, 1] - got[after, 2]) + (got[x, 2] - got[before, 1])
        residual = got[x, 0] - image
        first = residual * (1.0 / theta)
        out[x, 0] = residual
        out[x, 1] = first
        remain[x] = residual
        direction[0, x] = first
    for step in range(STEPS):
        now, later = step % 2, (step + 1) % 2
        rho_next = 1.0 / (2.0 * sigma - rho)
        flux_x = faces[planes - 1, 0] * (direction[now, planes - 1] - direction[now, 0])
        for x in range(planes):
            value = direction[now, x]
            flux_next = faces[x, 0] * (value - direction[now, (x + 1) % planes])
            applied = value + (flux_next - flux_x)
            flux_x = flux_next
            for axis in (0, 1):
                flux = faces[x, axis + 1] * (value - ahead(value, axis))
                applied = applied + (flux - behind(flux, axis))
            left = remain[x] - applied
            remain[x] = left
            new = (rho_next * rho) * value + (2.0 * rho_next / delta) * left
            direction[later, x] = new
            out[x, 1] = out[x, 1] + new
        rho = rho_next


def whole(memory):
    return pl.BlockSpec(memory_space=memory)


def kernel_of(body, outs, memories, scratch=(), flops=0, size=0, out_memory=VMEM):
    return pl.pallas_call(
        body,
        out_shape=outs,
        in_specs=[whole(m) for m in memories],
        out_specs=jax.tree.map(lambda _: whole(out_memory), outs),
        scratch_shapes=list(scratch),
        compiler_params=pltpu.CompilerParams(vmem_limit_bytes=8 << 20),
        cost_estimate=pl.CostEstimate(flops=flops, bytes_accessed=size, transcendentals=0),
    )


def f32(*shape):
    return jax.ShapeDtypeStruct(shape, jnp.float32)


def step(solution, source, mean_conductivity, kl_fields, couplings, mode_index):
    modes, _, ny, nz = solution.shape
    planes = lax.axis_size("gx")
    blocks = lax.axis_size("ma")
    chips = blocks // 2
    block = lax.axis_index("ma")
    core = block % 2
    sol = solution[:, 0]
    src = source[:, 0]
    mid = jnp.concatenate([mean_conductivity, kl_fields[:, 0]], 0)
    fields = mid.shape[0]

    def shifted(array, hops):
        pairs = []
        for x in range(planes):
            for y in range(blocks):
                target = (x + (hops if y % 2 == 0 else -hops)) % planes
                pairs.append((x * blocks + y, target * blocks + y))
        return lax.ppermute(array, ("gx", "ma"), pairs)

    def swapped(array):
        return lax.ppermute(array, "ma", [(i, i ^ 1) for i in range(blocks)])

    def ordered(mine, theirs):
        return jnp.where(core == 0, mine, theirs), jnp.where(core == 0, theirs, mine)

    mine = shifted(mid, 1)
    theirs = swapped(mine)

    same_core = [[2 * chip + c for chip in range(chips)] for c in range(2)]
    spread = jnp.broadcast_to(sol[None], (chips,) + sol.shape)
    near = lax.all_to_all(spread, "ma", 0, 0, tiled=True, axis_index_groups=same_core)
    far = swapped(near)

    rows = lax.dynamic_slice_in_dim(couplings, block * modes, modes, 1).transpose(0, 2, 1)
    own = block * modes + lax.broadcasted_iota(jnp.int32, rows.shape, 2)
    degree = lax.dynamic_slice_in_dim(mode_index, block * modes, modes, 0).T
    higher = degree[:, None, :] + (1 - lax.broadcasted_iota(jnp.int32, rows.shape, 1))
    weight = jnp.where(rows != own, jnp.sqrt(higher.astype(jnp.float32)), 0.0)
    owner = rows >> (modes.bit_length() - 1)
    is_near = (owner & 1) == core
    flat = (2 * (fields - 1), modes)
    index = ((owner >> 1) * modes + (rows & (modes - 1))).reshape(flat)
    near_weight = jnp.where(is_near, weight, 0.0).reshape(flat)
    far_weight = jnp.where(is_near, 0.0, weight).reshape(flat)

    tile = (ny, nz)
    cell = ny * nz
    pool = (chips * modes,) + tile
    faces = kernel_of(
        face_kernel, f32(fields, 6, *tile), [VMEM] * 3, flops=fields * 10 * cell, size=4 * cell * 9 * fields
    )(mid, mine, theirs)
    sums = kernel_of(
        near_kernel, f32(modes, 6, *tile), [SMEM] * 2 + [VMEM] * 2,
        flops=modes * fields * 16 * cell, size=4 * cell * (chips * modes + 8 * modes + 6 * fields),
    )(index, near_weight, near.reshape(pool), faces)
    mixed = kernel_of(
        far_kernel, f32(modes, 3, *tile), [SMEM] * 2 + [VMEM] * 5,
        [VMEM((modes, 3) + tile, jnp.float32), pltpu.SemaphoreType.DMA((modes // 2,))], out_memory=pl.ANY,
        flops=modes * fields * 16 * cell, size=4 * cell * (chips * modes + 11 * modes + 6 * fields),
    )(index, far_weight, far.reshape(pool), sol, src, sums, faces)
    down, up = ordered(mine[:1], theirs[:1])
    three = jnp.concatenate([down, mid[:1], up], 0)
    mean_mine = shifted(three, 3)
    mean_theirs = swapped(mean_mine)
    low, high = ordered(mean_mine, mean_theirs)
    nine = jnp.concatenate([low, three, high], 0)
    rest = shifted(nine[1:8], planes // 2)
    got = lax.all_to_all(mixed, "gx", 0, 0, tiled=True)
    done = kernel_of(
        cheb_kernel, f32(planes, 2, *tile), [VMEM] * 3,
        [VMEM((planes,) + tile, jnp.float32), VMEM((planes, 3) + tile, jnp.float32), VMEM((2, planes) + tile, jnp.float32), VMEM((planes,) + tile, jnp.float32)],
        flops=planes * STEPS * 30 * cell, size=4 * cell * planes * 6,
    )(got, nine, rest)
    back = lax.all_to_all(done, "gx", 0, 0, tiled=True)
    return (back[:, 0:1], back[:, 1:2])


def solution(mesh):
    in_specs = (
        P("ma", "gx", None, None),
        P("ma", "gx", None, None),
        P("gx", None, None),
        P(None, "gx", None, None),
        P(),
        P(),
    )
    out_specs = (P("ma", "gx", None, None), P("ma", "gx", None, None))
    return jax.shard_map(step, mesh=mesh, in_specs=in_specs, out_specs=out_specs, check_vma=False)
```

```python
import jax
import jax.numpy as jnp
from jax import lax
from jax.experimental import pallas as pl
from jax.experimental.pallas import tpu as pltpu
from jax.sharding import PartitionSpec as P

STEPS = 3
VMEM = pltpu.VMEM
SMEM = pltpu.SMEM


def ahead(a, axis):
    return pltpu.roll(a, a.shape[axis] - 1, axis)


def behind(a, axis):
    return pltpu.roll(a, 1, axis)


def mixture(index, weight, modes_in, k, i):
    mixed = None
    for s in range(2):
        at = 2 * k + s
        term = weight[at, i] * modes_in[index[at, i]]
        mixed = term if mixed is None else mixed + term
    return mixed


def face_kernel(mid, mine, theirs, faces):
    first = lax.rem(lax.axis_index("ma"), 2) == 0
    for q in range(mid.shape[0]):
        center = mid[q]
        faces[q, 0] = 0.5 * (center + jnp.where(first, theirs[q], mine[q]))
        faces[q, 1] = 0.5 * (center + jnp.where(first, mine[q], theirs[q]))
        for d, axis in ((2, 0), (4, 1)):
            face = 0.5 * (center + ahead(center, axis))
            faces[q, d] = face
            faces[q, d + 1] = behind(face, axis)


def add_mixtures(index, weight, pool, faces, rows, parts):
    for k in range(faces.shape[0] - 1):
        mixed = [mixture(index, weight, pool, k, i) for i in rows]
        for d in range(6):
            face = faces[k + 1, d]
            for n in range(len(rows)):
                parts[n][d] = parts[n][d] + face * mixed[n]
    return parts


def near_kernel(index, weight, near, faces, sums):
    modes = sums.shape[0]
    first = lax.div(lax.axis_index("ma"), 2) * modes

    @pl.loop(0, modes // 2, unroll=8)
    def _(pair):
        rows = (2 * pair, 2 * pair + 1)
        values = [near[first + i] for i in rows]
        parts = [[faces[0, d] * value for d in range(6)] for value in values]
        parts = add_mixtures(index, weight, near, faces, rows, parts)
        for n, i in enumerate(rows):
            for d in range(6):
                sums[i, d] = parts[n][d]


def far_kernel(index, weight, far, sol, src, sums, faces, out, held, sems):
    writes = []
    for pair in range(sol.shape[0] // 2):
        rows = (2 * pair, 2 * pair + 1)
        parts = [[sums[i, d] for d in range(6)] for i in rows]
        parts = add_mixtures(index, weight, far, faces, rows, parts)
        for n, i in enumerate(rows):
            image = sol[i]
            for d, axis in ((2, 0), (4, 1)):
                flux = parts[n][d] - ahead(parts[n][d + 1], axis)
                image = image + (flux - behind(flux, axis))
            held[i, 0] = src[i] - image
            held[i, 1] = parts[n][0]
            held[i, 2] = parts[n][1]
        slab = pl.ds(2 * pair, 2)
        writes.append(pltpu.make_async_copy(held.at[slab], out.at[slab], sems.at[pair]))
        writes[-1].start()
    for write in writes:
        write.wait()


def cheb_kernel(got, near_mean, far_mean, out, mean, faces, direction, remain):
    planes = got.shape[0]
    split = near_mean.shape[0]
    first = lax.axis_index("gx") + planes - 4
    for x in range(planes):
        mean[lax.rem(first + x, planes)] = near_mean[x] if x < split else far_mean[x - split]
    center = mean[0]
    for x in range(planes):
        after = mean[(x + 1) % planes]
        faces[x, 0] = 0.5 * (center + after)
        faces[x, 1] = 0.5 * (center + ahead(center, 0))
        faces[x, 2] = 0.5 * (center + ahead(center, 1))
        center = after
    theta = 13.0
    delta = 12.0
    sigma = theta / delta
    rho = 1.0 / sigma
    for x in range(planes):
        before, after = (x - 1) % planes, (x + 1) % planes
        image = (got[x, 1] - got[after, 2]) + (got[x, 2] - got[before, 1])
        residual = got[x, 0] - image
        first = residual * (1.0 / theta)
        out[x, 0] = residual
        remain[x] = residual
        direction[0, x] = first
    for step in range(STEPS):
        now, later = step, step + 1
        rho_next = 1.0 / (2.0 * sigma - rho)
        flux_x = faces[planes - 1, 0] * (direction[now, planes - 1] - direction[now, 0])
        for x in range(planes):
            value = direction[now, x]
            flux_next = faces[x, 0] * (value - direction[now, (x + 1) % planes])
            applied = value + (flux_next - flux_x)
            flux_x = flux_next
            for axis in (0, 1):
                flux = faces[x, axis + 1] * (value - ahead(value, axis))
                applied = applied + (flux - behind(flux, axis))
            left = remain[x] - applied
            remain[x] = left
            new = (rho_next * rho) * value + (2.0 * rho_next / delta) * left
            if step < STEPS - 1:
                direction[later, x] = new
            else:
                total = direction[0, x]
                for past in range(1, STEPS):
                    total = total + direction[past, x]
                out[x, 1] = total + new
        rho = rho_next


def whole(memory):
    return pl.BlockSpec(memory_space=memory)


def kernel_of(body, outs, memories, scratch=(), flops=0, size=0, out_memory=VMEM):
    return pl.pallas_call(
        body,
        out_shape=outs,
        in_specs=[whole(m) for m in memories],
        out_specs=jax.tree.map(lambda _: whole(out_memory), outs),
        scratch_shapes=list(scratch),
        compiler_params=pltpu.CompilerParams(vmem_limit_bytes=8 << 20),
        cost_estimate=pl.CostEstimate(flops=flops, bytes_accessed=size, transcendentals=0),
    )


def f32(*shape):
    return jax.ShapeDtypeStruct(shape, jnp.float32)


def step(solution, source, mean_conductivity, kl_fields, couplings, mode_index):
    modes, _, ny, nz = solution.shape
    planes = lax.axis_size("gx")
    blocks = lax.axis_size("ma")
    chips = blocks // 2
    block = lax.axis_index("ma")
    core = block % 2
    sol = solution[:, 0]
    src = source[:, 0]
    mid = jnp.concatenate([mean_conductivity, kl_fields[:, 0]], 0)
    fields = mid.shape[0]

    def shifted(array, hops):
        pairs = []
        for x in range(planes):
            for y in range(blocks):
                target = (x + (hops if y % 2 == 0 else -hops)) % planes
                pairs.append((x * blocks + y, target * blocks + y))
        return lax.ppermute(array, ("gx", "ma"), pairs)

    def swapped(array):
        return lax.ppermute(array, "ma", [(i, i ^ 1) for i in range(blocks)])

    def ordered(mine, theirs):
        return jnp.where(core == 0, mine, theirs), jnp.where(core == 0, theirs, mine)

    mine = shifted(mid, 1)
    theirs = swapped(mine)

    same_core = [[2 * chip + c for chip in range(chips)] for c in range(2)]
    spread = jnp.broadcast_to(sol[None], (chips,) + sol.shape)
    near = lax.all_to_all(spread, "ma", 0, 0, tiled=True, axis_index_groups=same_core)
    far = swapped(near)

    rows = lax.dynamic_slice_in_dim(couplings, block * modes, modes, 1).transpose(0, 2, 1)
    own = block * modes + lax.broadcasted_iota(jnp.int32, rows.shape, 2)
    degree = lax.dynamic_slice_in_dim(mode_index, block * modes, modes, 0).T
    higher = degree[:, None, :] + (1 - lax.broadcasted_iota(jnp.int32, rows.shape, 1))
    weight = jnp.where(rows != own, jnp.sqrt(higher.astype(jnp.float32)), 0.0)
    owner = rows >> (modes.bit_length() - 1)
    is_near = (owner & 1) == core
    flat = (2 * (fields - 1), modes)
    index = ((owner >> 1) * modes + (rows & (modes - 1))).reshape(flat)
    near_weight = jnp.where(is_near, weight, 0.0).reshape(flat)
    far_weight = jnp.where(is_near, 0.0, weight).reshape(flat)

    tile = (ny, nz)
    cell = ny * nz
    pool = (chips * modes,) + tile
    faces = kernel_of(
        face_kernel, f32(fields, 6, *tile), [VMEM] * 3, flops=fields * 10 * cell, size=4 * cell * 9 * fields
    )(mid, mine, theirs)
    sums = kernel_of(
        near_kernel, f32(modes, 6, *tile), [SMEM] * 2 + [VMEM] * 2,
        flops=modes * fields * 16 * cell, size=4 * cell * (chips * modes + 8 * modes + 6 * fields),
    )(index, near_weight, near.reshape(pool), faces)
    mixed = kernel_of(
        far_kernel, f32(modes, 3, *tile), [SMEM] * 2 + [VMEM] * 5,
        [VMEM((modes, 3) + tile, jnp.float32), pltpu.SemaphoreType.DMA((modes // 2,))], out_memory=pl.ANY,
        flops=modes * fields * 16 * cell, size=4 * cell * (chips * modes + 11 * modes + 6 * fields),
    )(index, far_weight, far.reshape(pool), sol, src, sums, faces)
    down, up = ordered(mine[:1], theirs[:1])
    three = jnp.concatenate([down, mid[:1], up], 0)
    mean_mine = shifted(three, 3)
    mean_theirs = swapped(mean_mine)
    low, high = ordered(mean_mine, mean_theirs)
    nine = jnp.concatenate([low, three, high], 0)
    rest = shifted(nine[1:8], planes // 2)
    got = lax.all_to_all(mixed, "gx", 0, 0, tiled=True)
    done = kernel_of(
        cheb_kernel, f32(planes, 2, *tile), [VMEM] * 3,
        [VMEM((planes,) + tile, jnp.float32), VMEM((planes, 3) + tile, jnp.float32), VMEM((STEPS, planes) + tile, jnp.float32), VMEM((planes,) + tile, jnp.float32)],
        flops=planes * STEPS * 30 * cell, size=4 * cell * planes * 6,
    )(got, nine, rest)
    back = lax.all_to_all(done, "gx", 0, 0, tiled=True)
    return (back[:, 0:1], back[:, 1:2])


def solution(mesh):
    in_specs = (
        P("ma", "gx", None, None),
        P("ma", "gx", None, None),
        P("gx", None, None),
        P(None, "gx", None, None),
        P(),
        P(),
    )
    out_specs = (P("ma", "gx", None, None), P("ma", "gx", None, None))
    return jax.shard_map(step, mesh=mesh, in_specs=in_specs, out_specs=out_specs, check_vma=False)
```
